256 devices in a mesh: dp: 64 (over z, y, core), tensor: 4 (over x).
Axes of the slice: x: 4, y: 4, z: 8, core: 2. Of those that a mesh axis runs over, the one named last changes fastest.
Arguments:
- queries: bfloat16 [32768, 2048], P('dp', 'tensor'), may hold values from -360 to 360
- neighbours: int32 [512, 2], P('dp'), may hold values from 0 to 63, as said below
- counts: int32 [512], P('dp'), may hold values from 1 to 2
- states: bfloat16 [64, 128, 4096], P('dp'), may hold values from -6 to 6
- w_key: bfloat16 [4096, 2048], P('dp', 'tensor'), may hold values from -0.09375 to 0.09375
- w_value: bfloat16 [4096, 2048], P('dp', 'tensor'), may hold values from -0.09375 to 0.09375
- cotangent: bfloat16 [32768, 2048], P('dp', 'tensor'), may hold values from -6 to 6
Outputs:
- context: bfloat16 [32768, 2048], P('dp', 'tensor')
- query_grad: bfloat16 [32768, 2048], P('dp', 'tensor')
- state_grad: bfloat16 [64, 128, 4096], P('dp', None, 'tensor')
The draws below stay inside these ranges and needn't reach their ends.
Inputs may be any that keep to these rules, and one draw needn't show every extreme that they name: Neighbour n is held by dp index n. Among the 16 slots of one index of dp, at most 1 name neighbours of one holder, and some holder is named exactly 1 times.
All inputs are finite; a program needn't handle non-finite values.
Results may differ from the reference program's by a relative error of at most 0.035.
The reference program's roundings to bfloat16 on the way count: a program that leaves them out, or rounds other values in their place, can miss the bound.
Values may be sent and summed in bfloat16 or wider, within the bound.
A program may use at most 128 MiB of HBM per device.

```python
import math
import jax
import jax.numpy as jnp
from jax import lax

D = 4096
HEADS = 16
HEAD = 128
CQ = 64
NL = 128
NEIGH = 2
SPANS = 8
NBR_DEV = 1
OWNERS = 64
NBRS = 64
NCHUNKS = 512
TOKENS = 32768
N_DP = 64
N_TENSOR = 4


def draw_neighbours(key, part):
    key_hot, key_noise, key_local = jax.random.split(key, 3)
    hot_level = jax.random.randint(key_hot, (OWNERS,), 0, 64)
    noise_level = jax.random.randint(key_noise, (OWNERS, OWNERS), 0, 64)
    priority = (hot_level[None, :] + noise_level) * OWNERS + jnp.arange(OWNERS, dtype=jnp.int32)[None, :]
    ranking = jnp.argsort(-priority, axis=1, stable=True).astype(jnp.int32)
    slot_pos = jnp.arange(SPANS * NEIGH, dtype=jnp.int32) % OWNERS
    holder = ranking[:, slot_pos]
    local_index = jax.random.randint(key_local, (OWNERS, SPANS * NEIGH), 0, NBR_DEV)
    return (holder * NBR_DEV + local_index).reshape(OWNERS * SPANS, NEIGH).astype(jnp.int32)


def draw_queries(key, part):
    key_base = jax.random.fold_in(key, 0)
    base = jax.random.truncated_normal(key_base, -6.0, 6.0, (TOKENS, HEADS * HEAD), jnp.float32)
    return base.astype(jnp.bfloat16)


def set_ends(values, rng, smallest, largest):
    extent = values.shape
    place = [jax.random.randint(jax.random.fold_in(rng, axis), (), 0, extent[axis]) for axis in range(len(extent))]
    values = values.at[tuple(place)].set(smallest)
    longest = extent.index(max(extent))
    place[longest] = (place[longest] + 1) % extent[longest]
    return values.at[tuple(place)].set(largest)


def levels(rng, shape, cuts, low, top_value):
    level = 1.0
    for dim, blocks in cuts:
        heights = jax.random.uniform(jax.random.fold_in(jax.random.fold_in(rng, 6), dim), (blocks,), jnp.float32, low / len(cuts), top_value / len(cuts))
        level = level * jnp.repeat(jnp.exp(heights), shape[dim] // blocks).reshape((-1,) + (1,) * (len(shape) - 1 - dim))
    return level


def scatter_about(own_key, dims, width, most, pieces=(), held_as=jnp.bfloat16):
    values = jax.random.normal(own_key, dims, jnp.float32) * width
    if len(pieces) > 0:
        values = levels(own_key, dims, pieces, -0.22, 0.18) * values
    return jnp.clip(values, min=-most, max=most).astype(held_as)


def setup_inputs(seed: int = 0) -> dict:
    arg_keys = jax.random.split(jax.random.key(seed), 8)
    queries = draw_queries(jax.random.fold_in(arg_keys[7], 71), 0)
    neighbours = draw_neighbours(jax.random.fold_in(arg_keys[7], 71), 0)
    counts = set_ends(jax.random.randint(arg_keys[2], (NCHUNKS,), 1, NEIGH + 1), jax.random.fold_in(arg_keys[2], 1), 1, NEIGH).astype(jnp.int32)
    states = scatter_about(arg_keys[3], (NBRS, NL, D), 1.0, 6.0, ((0, 64),))
    w_key = scatter_about(arg_keys[4], (D, HEADS * HEAD), D ** -0.5, 0.09375, ((0, 64), (1, 4)))
    w_value = scatter_about(arg_keys[5], (D, HEADS * HEAD), D ** -0.5, 0.09375, ((0, 64), (1, 4)))
    cotangent = scatter_about(arg_keys[6], (TOKENS, HEADS * HEAD), 1.0, 6.0, ((0, 64), (1, 4)))
    return dict(queries=queries, neighbours=neighbours, counts=counts, states=states, w_key=w_key, w_value=w_value, cotangent=cotangent)


def rounded(x):
    return lax.optimization_barrier(x.astype(jnp.bfloat16)).astype(jnp.float32)

def reference(queries, neighbours, counts, states, w_key, w_value, cotangent):
    score_scale = 1.0 / math.sqrt(HEAD)
    flat_states = states.reshape(NBRS * NL, D)
    key_rows = jnp.dot(flat_states, w_key, preferred_element_type=jnp.float32).astype(jnp.bfloat16).reshape(NBRS, NL, HEADS, HEAD)
    value_rows = jnp.dot(flat_states, w_value, preferred_element_type=jnp.float32).astype(jnp.bfloat16).reshape(NBRS, NL, HEADS, HEAD)
    inputs = (queries.reshape(N_DP, SPANS, CQ, HEADS, HEAD), cotangent.reshape(N_DP, SPANS, CQ, HEADS, HEAD), neighbours.reshape(N_DP, SPANS, NEIGH).astype(jnp.int32), counts.reshape(N_DP, SPANS).astype(jnp.int32))

    def one_block(carried, block_in):
        key_acc, value_acc = carried
        query_blk, grad_blk, id_blk, count_blk = block_in
        key_sel = key_rows[id_blk].astype(jnp.float32)
        value_sel = value_rows[id_blk].astype(jnp.float32)
        query_f = query_blk.astype(jnp.float32)
        scores = jnp.einsum('cqhd,cjkhd->cjhqk', query_f, key_sel) * score_scale
        row_max = lax.optimization_barrier(jnp.max(scores, axis=-1, keepdims=True))
        log_total = row_max[..., 0] + jnp.log(lax.optimization_barrier(jnp.sum(jnp.exp(scores - row_max), axis=-1)))
        prob_rows = jnp.exp(scores - log_total[..., None])
        prob_half = rounded(prob_rows)
        partial_value = rounded(jnp.einsum('cjhqk,cjkhd->cjqhd', prob_half, value_sel))
        log_part = jnp.transpose(log_total, (0, 1, 3, 2))
        is_valid = jnp.arange(NEIGH, dtype=jnp.int32)[None, :] < count_blk[:, None]
        live = is_valid[:, :, None, None]
        masked = jnp.where(live, log_part, -1e+30)
        top_part = lax.optimization_barrier(jnp.max(masked, axis=1, keepdims=True))
        raw_weight = jnp.where(live, jnp.exp(masked - top_part), 0.0)
        mix_weight = raw_weight / lax.optimization_barrier(jnp.sum(raw_weight, axis=1, keepdims=True))
        mixed_rows = lax.optimization_barrier(jnp.sum(mix_weight[..., None] * partial_value, axis=1))
        grad_rows = grad_blk.astype(jnp.float32)
        part_grad = rounded(mix_weight[..., None] * grad_rows[:, None])
        lse_grad = mix_weight * lax.optimization_barrier(jnp.sum(grad_rows[:, None] * (partial_value - mixed_rows[:, None]), axis=-1))
        rest_term = lax.optimization_barrier(jnp.sum(part_grad * partial_value, axis=-1)) - lse_grad
        dprob = jnp.einsum('cjqhd,cjkhd->cjhqk', part_grad, value_sel)
        dscore = prob_rows * (dprob - jnp.transpose(rest_term, (0, 1, 3, 2))[..., None])
        dscore_half = rounded(dscore)
        slot_dq = rounded(jnp.einsum('cjhqk,cjkhd->cjqhd', dscore_half, key_sel) * score_scale)
        query_grad = lax.optimization_barrier(jnp.sum(slot_dq, axis=1)).astype(jnp.bfloat16)
        slot_dk = jnp.einsum('cjhqk,cqhd->cjkhd', dscore_half, query_f) * score_scale
        slot_dv = jnp.einsum('cjhqk,cjqhd->cjkhd', prob_half, part_grad)
        flat_ids = id_blk.reshape(SPANS * NEIGH)
        key_acc = key_acc.at[flat_ids].add(slot_dk.reshape(SPANS * NEIGH, NL, HEADS, HEAD))
        value_acc = value_acc.at[flat_ids].add(slot_dv.reshape(SPANS * NEIGH, NL, HEADS, HEAD))
        return ((key_acc, value_acc), (mixed_rows.astype(jnp.bfloat16), query_grad))
    start_acc = jnp.zeros((NBRS, NL, HEADS, HEAD), jnp.float32)
    (key_acc, value_acc), (context, query_grad) = lax.scan(one_block, (start_acc, start_acc), inputs)
    key_grad = key_acc.astype(jnp.bfloat16).reshape(NBRS * NL, HEADS * HEAD)
    value_grad = value_acc.astype(jnp.bfloat16).reshape(NBRS * NL, HEADS * HEAD)
    group_width = HEADS * HEAD // N_TENSOR
    total_sum = jnp.zeros((NBRS * NL, D), jnp.float32)
    for group in range(N_TENSOR):
        first_col = group * group_width
        term = jnp.dot(key_grad[:, first_col:first_col + group_width], w_key[:, first_col:first_col + group_width].T, preferred_element_type=jnp.float32)
        term = term + jnp.dot(value_grad[:, first_col:first_col + group_width], w_value[:, first_col:first_col + group_width].T, preferred_element_type=jnp.float32)
        total_sum = total_sum + rounded(term)
    state_grad = total_sum.astype(jnp.bfloat16).reshape(NBRS, NL, D)
    return (context.reshape(TOKENS, HEADS * HEAD), query_grad.reshape(TOKENS, HEADS * HEAD), state_grad)
```

```python
import functools
import math

import jax
import jax.numpy as jnp
from jax import lax
from jax.experimental import pallas as pl
from jax.experimental.pallas import tpu as pltpu
from jax.sharding import PartitionSpec as P

HEAD = 128
NT = (((1,), (1,)), ((), ()))
TN = (((0,), (0,)), ((), ()))


def dot(a, b, dims=(((1,), (0,)), ((), ()))):
    return lax.dot_general(a, b, dims, preferred_element_type=jnp.float32)


def span_head(q, g, k, v, live):
    scale = 1.0 / math.sqrt(HEAD)
    prob, log_total, part = [], [], []
    for j in range(2):
        s = dot(q, k[j], NT) * scale
        m = jnp.max(s, axis=-1, keepdims=True)
        e = jnp.exp(s - m)
        total = jnp.sum(e, axis=-1, keepdims=True)
        prob.append(e * (1.0 / total))
        log_total.append(m + jnp.log(total))
    half = [p.astype(jnp.bfloat16) for p in prob]
    part = [dot(half[j], v[j]).astype(jnp.bfloat16).astype(jnp.float32) for j in range(2)]
    other = jnp.where(live, log_total[1], -1e30)
    top = jnp.maximum(log_total[0], other)
    raw = [jnp.exp(log_total[0] - top), jnp.where(live, jnp.exp(other - top), 0.0)]
    norm = 1.0 / (raw[0] + raw[1])
    mix = [r * norm for r in raw]
    mixed = mix[0] * part[0] + mix[1] * part[1]
    gf = g.astype(jnp.float32)
    dq = None
    dk, dv = [], []
    for j in range(2):
        pg = (mix[j] * gf).astype(jnp.bfloat16)
        lse = mix[j] * jnp.sum(gf * (part[j] - mixed), axis=-1, keepdims=True)
        rest = jnp.sum(pg.astype(jnp.float32) * part[j], axis=-1, keepdims=True) - lse
        ds = (prob[j] * (dot(pg, v[j], NT) - rest)).astype(jnp.bfloat16)
        one = (dot(ds, k[j]) * scale).astype(jnp.bfloat16).astype(jnp.float32)
        dq = one if dq is None else dq + one
        dk.append((dot(ds, q, TN) * scale).astype(jnp.bfloat16))
        dv.append(dot(half[j], pg, TN).astype(jnp.bfloat16))
    return mixed.astype(jnp.bfloat16), dq.astype(jnp.bfloat16), dk, dv


def attend(ids, counts, q_ref, g_ref, kv_hbm, ctx_ref, dq_ref, dkv_hbm, kv, dkv, zero, named, in_sem, out_sem, zero_sem):
    slots = ids.shape[0]
    spans = slots // 2
    rows = q_ref.shape[0] // spans
    width = q_ref.shape[1]
    owners = kv_hbm.shape[0]

    def load(s):
        return pltpu.make_async_copy(kv_hbm.at[ids[s]], kv.at[s], in_sem.at[s])

    def store(s):
        return pltpu.make_async_copy(dkv.at[s], dkv_hbm.at[ids[s]], out_sem.at[s])

    for s in range(slots):
        load(s).start()
    zero[...] = jnp.zeros_like(zero)

    @pl.loop(0, owners)
    def _(n):
        named[n] = 0

    for s in range(slots):
        named[ids[s]] = 1

    @pl.loop(0, owners)
    def _(n):
        @pl.when(named[n] == 0)
        def _():
            pltpu.make_async_copy(zero, dkv_hbm.at[n], zero_sem).start()

    @pl.loop(0, spans)
    def _(c):
        load(2 * c).wait()
        load(2 * c + 1).wait()
        live = counts[c] > 1
        span = pl.ds(pl.multiple_of(c * rows, rows), rows)
        for h in range(width // HEAD):
            cols = slice(h * HEAD, (h + 1) * HEAD)
            vcols = slice(width + h * HEAD, width + (h + 1) * HEAD)
            k = [kv[2 * c + j, :, cols] for j in range(2)]
            v = [kv[2 * c + j, :, vcols] for j in range(2)]
            ctx, dq, dk, dv = span_head(q_ref[span, cols], g_ref[span, cols], k, v, live)
            ctx_ref[span, cols] = ctx
            dq_ref[span, cols] = dq
            for j in range(2):
                dkv[2 * c + j, :, cols] = dk[j]
                dkv[2 * c + j, :, vcols] = dv[j]
        store(2 * c).start()
        store(2 * c + 1).start()

    for s in range(slots):
        store(s).wait()
    rest = dkv_hbm.at[pl.ds(0, owners - slots)]
    pltpu.make_async_copy(rest, rest, zero_sem).wait()


def local(queries, neighbours, counts, states, w_key, w_value, cotangent):
    owners = lax.axis_size("dp")
    spans, neigh = neighbours.shape
    slots = spans * neigh
    tokens, width = queries.shape
    _, rows, dmodel = states.shape
    w_all = lax.all_gather(jnp.concatenate([w_key, w_value], axis=1), "dp", axis=0, tiled=True)
    kv_own = dot(states.reshape(rows, dmodel), w_all).astype(jnp.bfloat16)
    kv_all = lax.all_gather(kv_own, "dp", axis=0, tiled=False)
    vmem = pl.BlockSpec(memory_space=pltpu.VMEM)
    smem = pl.BlockSpec(memory_space=pltpu.SMEM)
    hbm = pl.BlockSpec(memory_space=pl.ANY)
    context, query_grad, dkv_all = pl.pallas_call(
        attend,
        out_shape=(
            jax.ShapeDtypeStruct((tokens, width), jnp.bfloat16),
            jax.ShapeDtypeStruct((tokens, width), jnp.bfloat16),
            jax.ShapeDtypeStruct((owners, rows, 2 * width), jnp.bfloat16),
        ),
        in_specs=[smem, smem, vmem, vmem, hbm],
        out_specs=(vmem, vmem, hbm),
        scratch_shapes=[
            pltpu.VMEM((slots, rows, 2 * width), jnp.bfloat16),
            pltpu.VMEM((slots, rows, 2 * width), jnp.bfloat16),
            pltpu.VMEM((rows, 2 * width), jnp.bfloat16),
            pltpu.SMEM((owners,), jnp.int32),
            pltpu.SemaphoreType.DMA((slots,)),
            pltpu.SemaphoreType.DMA((slots,)),
            pltpu.SemaphoreType.DMA,
        ],
        compiler_params=pltpu.CompilerParams(vmem_limit_bytes=32 << 20),
        name="attend",
    )(neighbours.reshape(slots), counts, queries, cotangent, kv_all)
    dkv = lax.psum_scatter(dkv_all.reshape(owners * rows, 2 * width), "dp", scatter_dimension=0, tiled=True)
    term = dot(dkv, w_all, NT).astype(jnp.bfloat16)
    state_grad = lax.psum_scatter(term, "tensor", scatter_dimension=1, tiled=True)
    return context, query_grad, state_grad.reshape(1, rows, state_grad.shape[1])


def solution(mesh):
    placed = (
        P("dp", "tensor"),
        P("dp", None),
        P("dp"),
        P("dp", None, None),
        P("dp", "tensor"),
        P("dp", "tensor"),
        P("dp", "tensor"),
    )
    return jax.shard_map(
        local,
        mesh=mesh,
        in_specs=placed,
        out_specs=(P("dp", "tensor"), P("dp", "tensor"), P("dp", None, "tensor")),
        check_vma=False,
    )
```
